32 devices in a mesh: ctx: 8 (over z, x), head: 4 (over y, core).
Axes of the slice: x: 2, y: 2, z: 4, core: 2. Of those that a mesh axis runs over, the one named last changes fastest.
Arguments:
- queries: bfloat16 [8192, 512], P('ctx', 'head'), may hold values from -6 to 6
- keys: bfloat16 [8192, 512], P('ctx', 'head'), may hold values from -6 to 6
- values: bfloat16 [8192, 512], P('ctx', 'head'), may hold values from -6 to 6
- write_rates: float32 [4, 8192], P('head', 'ctx'), may hold values from 0 to 2, as said below
- norm_gain: float32 [128], replicated, may hold values from 0.1 to 1.9
- w_out: bfloat16 [512, 2048], P(None, 'head'), may hold values from -0.25 to 0.25
Outputs:
- mixed: bfloat16 [8192, 2048], P('ctx', 'head')
The draws below stay inside these ranges and needn't reach their ends.
Inputs may be any that keep to these rules, and one draw needn't show every extreme that they name: `write_rates`: every rate lies strictly between 0 and 2.
All inputs are finite; a program needn't handle non-finite values.
Results may differ from the reference program's by a relative error of at most 0.0049.
Values may be sent and summed in bfloat16 or wider, within the bound.
A program may use at most 64 MiB of HBM per device.

```python
import jax
import jax.numpy as jnp
from jax import lax

D = 2048
HEAD_DIM = 128
GROUP = 128
HEADS = 4
TOKENS = 8192


def draw_write_rates(key, part):
    first, second, third = jax.random.split(jax.random.fold_in(key, 7), 3)
    kinds = jax.random.randint(first, (HEADS, 1), 0, 3)
    small = HEAD_DIM / TOKENS * jnp.exp(jax.random.uniform(second, (HEADS, TOKENS), jnp.float32, jnp.log(0.25), 0.0))
    strong = jax.random.uniform(third, (HEADS, TOKENS), jnp.float32, 0.3, 1.7)
    rates = jnp.where(kinds == 0, small, jnp.where(kinds == 1, 2.0 - small, strong))
    return rates.astype(jnp.float32)


def block_levels(own_key, dims, cuts, least, high):
    gain, own = 1.0, jax.random.fold_in(own_key, 6)
    for axis_at, shards_of in cuts:
        steps = jnp.exp(jax.random.uniform(jax.random.fold_in(own, axis_at), (shards_of,), jnp.float32, least / len(cuts), high / len(cuts)))
        gain = gain * jnp.repeat(steps, dims[axis_at] // shards_of).reshape([-1 if axis == axis_at else 1 for axis in range(len(dims))])
    return gain


def gaussian(rng, dims, scale, reach, cuts=(), kind=jnp.bfloat16):
    factor_of = block_levels(rng, dims, cuts, -0.22, 0.18) if cuts else 1.0
    values = jax.random.normal(rng, dims, jnp.float32) * scale * factor_of
    return jnp.minimum(jnp.maximum(values, -reach), reach).astype(kind)


def setup_inputs(seed: int = 0) -> dict:
    streams_of = jax.random.split(jax.random.key(seed), 7)
    return {
        "queries": gaussian(streams_of[0], (TOKENS, HEADS * HEAD_DIM), 1.0, 6.0, ((0, 8), (1, 4))),
        "keys": gaussian(streams_of[1], (TOKENS, HEADS * HEAD_DIM), 1.0, 6.0, ((0, 8), (1, 4))),
        "values": gaussian(streams_of[2], (TOKENS, HEADS * HEAD_DIM), 1.0, 6.0, ((0, 8), (1, 4))),
        "write_rates": draw_write_rates(jax.random.fold_in(streams_of[6], 71), 0),
        "norm_gain": jnp.clip(1.0 + 0.18 * jax.random.normal(streams_of[4], (HEAD_DIM,), jnp.float32), 0.1, 1.9),
        "w_out": gaussian(streams_of[5], (HEADS * HEAD_DIM, D), (HEADS * HEAD_DIM) ** -0.5, 0.25, ((1, 4),)),
    }


def matmul(left, right):
    return jnp.dot(left.astype(jnp.float32), right.astype(jnp.float32), precision=lax.Precision.HIGHEST, preferred_element_type=jnp.float32)

def unit_rows(matrix):
    wide = matrix.astype(jnp.float32)
    return wide / jnp.sqrt(lax.optimization_barrier(jnp.sum(wide * wide, axis=-1, keepdims=True)) + 1e-06)

def block_parts(query_block, key_block, value_block, rate_block):
    width = key_block.shape[1]
    gram = matmul(key_block, key_block.T)
    lower = jnp.tril(rate_block[:, None] * gram, -1) + jnp.eye(key_block.shape[0], dtype=jnp.float32)
    stacked = jnp.concatenate([rate_block[:, None] * key_block, rate_block[:, None] * value_block], axis=1)
    solved = jax.scipy.linalg.solve_triangular(lower, stacked, lower=True, unit_diagonal=True)
    wy_keys = solved[:, :width]
    wy_values = solved[:, width:]
    transition = jnp.eye(width, dtype=jnp.float32) - matmul(wy_keys.T, key_block)
    offset = matmul(wy_values.T, key_block)
    scores = jnp.tril(matmul(query_block, key_block.T))
    return (wy_keys, wy_values, transition, offset, scores)

def block_output(state, query_block, wy_keys, wy_values, transition, offset, scores):
    result = matmul(query_block, state.T) + matmul(scores, wy_values - matmul(wy_keys, state.T))
    return (result, matmul(state, transition) + offset)

def head_run(inputs):
    query_head, key_head, value_head, rate_head = inputs
    blocks = query_head.shape[0] // GROUP

    def advance(state, block):
        pieces = block_parts(block[0], block[1], block[2], block[3])
        result, state = block_output(state, block[0], *pieces)
        return (state, result)
    start_state = jnp.zeros((HEAD_DIM, HEAD_DIM), jnp.float32)
    final, outputs = lax.scan(advance, start_state, (query_head.reshape(blocks, GROUP, HEAD_DIM), key_head.reshape(blocks, GROUP, HEAD_DIM), value_head.reshape(blocks, GROUP, HEAD_DIM), rate_head.reshape(blocks, GROUP)))
    return outputs.reshape(-1, HEAD_DIM)

def reference(queries, keys, values, write_rates, norm_gain, w_out):
    length = queries.shape[0]
    heads = queries.shape[1] // HEAD_DIM
    query_heads = unit_rows(queries.reshape(length, heads, HEAD_DIM)).transpose(1, 0, 2)
    key_heads = unit_rows(keys.reshape(length, heads, HEAD_DIM)).transpose(1, 0, 2)
    value_heads = values.astype(jnp.float32).reshape(length, heads, HEAD_DIM).transpose(1, 0, 2)
    outputs = lax.map(head_run, (query_heads, key_heads, value_heads, write_rates.astype(jnp.float32)))
    normed = outputs * lax.rsqrt(lax.optimization_barrier(jnp.mean(outputs * outputs, axis=-1, keepdims=True)) + 1e-06) * norm_gain
    normed = normed.astype(jnp.bfloat16).transpose(1, 0, 2).reshape(length, heads * HEAD_DIM)
    return jnp.dot(normed.astype(jnp.float32), w_out.astype(jnp.float32), preferred_element_type=jnp.float32).astype(jnp.bfloat16)
```

```python
import functools

import jax
import jax.numpy as jnp
from jax import lax
from jax.experimental import pallas as pl
from jax.experimental.pallas import tpu as pltpu
from jax.sharding import PartitionSpec as P

F32 = jnp.float32
BF16 = jnp.bfloat16
MESH = pl.DeviceIdType.MESH
GROUP = 128
CHUNKS = 4


def halves(wide):
    high = wide.astype(BF16)
    return high, (wide - high.astype(F32)).astype(BF16)


def dot(left, right):
    return jnp.dot(left, right, preferred_element_type=F32)


def dot_rows(left, right):
    return lax.dot_general(left, right, (((1,), (1,)), ((), ())), preferred_element_type=F32)


def beside(*parts):
    return jnp.concatenate(parts, axis=1)


def above(*parts):
    return jnp.concatenate(parts, axis=0)


def dot_wide(left, right):
    left_high, left_low = halves(left)
    right_high, right_low = halves(right)
    return dot(beside(left_high, left_low, left_high), above(right_high, right_high, right_low))


def kernel(
    count,
    heads,
    q_ref,
    k_ref,
    v_ref,
    rate_ref,
    gain_ref,
    w_ref,
    out_ref,
    inverse,
    lower,
    writes,
    moves,
    prefix,
    eff_high,
    eff_low,
    local,
    pair,
    state_in,
    state_out,
    gathered,
    pair_send,
    pair_recv,
    state_send,
    state_recv,
    out_send,
    forward_send,
    out_recv,
):
    ctx = lax.axis_index("ctx")
    head = lax.axis_index("head")
    side = lax.rem(ctx, 2)
    place = ctx // 2
    places = count // 2
    mate = ctx + 1 - 2 * side
    core = lax.rem(head, 2)
    chip = head // 2
    chips = heads // 2
    twin = head + 1 - 2 * core
    length, width = q_ref.shape
    blocks = length // GROUP

    barrier = pltpu.get_barrier_semaphore()

    def greet(to_ctx, to_head):
        pl.semaphore_signal(barrier, inc=1, device_id=(to_ctx, to_head), device_id_type=MESH)

    def chip_at(step):
        return lax.rem(chip + step, chips)

    greet(mate, head)
    greet(ctx, twin)
    for step in range(1, chips):
        greet(ctx, chip_at(step) * 2 + core)

    @pl.when(place > 0)
    def _():
        greet(ctx - 2, head)

    @pl.when(place < places - 1)
    def _():
        greet(ctx + 2, head)

    row = lax.broadcasted_iota(jnp.int32, (GROUP, GROUP), 0)
    col = lax.broadcasted_iota(jnp.int32, (GROUP, GROUP), 1)
    eye = (row == col).astype(F32)

    rates = above(*[rate_ref[0:1, b * GROUP : (b + 1) * GROUP] for b in range(blocks)])
    rate_cols = rates.T
    key_rows = []

    def part(ref, b):
        return ref[b * GROUP : (b + 1) * GROUP, :]

    for b in range(blocks):
        key = part(k_ref, b)
        wide = key.astype(F32)
        gram = dot_rows(key, key)
        scale_col = lax.rsqrt(jnp.sum(wide * wide, axis=1, keepdims=True) + 1e-06)
        scale_row = lax.rsqrt(jnp.sum(gram * eye, axis=0, keepdims=True) + 1e-06)
        key_rows.append(scale_row)
        strict = jnp.where(
            row > col, gram * (rate_cols[:, b : b + 1] * scale_col) * scale_row, 0.0
        )
        lower[b] = strict
        near = (row // 2 == col // 2) & (row != col)
        inverse[b] = eye - jnp.where(near, strict, 0.0)

    span = 2
    while span < GROUP:
        corner = (row // (2 * span) == col // (2 * span)) & (row // span != col // span)
        for b in range(blocks):
            held = inverse[b]
            inverse[b] = held - dot_wide(
                held, dot_wide(jnp.where(corner, lower[b], 0.0), held)
            )
        span *= 2

    for b in range(blocks):
        key = part(k_ref, b)
        value = part(v_ref, b)
        wide = key.astype(F32)
        scale_col = lax.rsqrt(jnp.sum(wide * wide, axis=1, keepdims=True) + 1e-06)
        spread = inverse[b] * rates[b : b + 1, :]
        key_high, key_low = halves(spread * key_rows[b])
        value_high, value_low = halves(spread)
        written = beside(
            dot(beside(key_high, key_low), above(key, key)),
            dot(beside(value_high, value_low), above(value, value)),
        )
        writes[b] = written
        high, low = halves(written * scale_col)
        turned = key.T
        moved = dot(beside(turned, turned), above(high, low))
        moves[b] = beside(eye - moved[:, :width], moved[:, width:])

    nothing = jnp.zeros((GROUP, width), F32)
    run = beside(eye, nothing)
    for b in range(blocks):
        prefix[b] = run
        step = moves[b]
        if b == 0:
            run = step
        else:
            run = dot_wide(step[:, :width], run) + beside(nothing, step[:, width:])
    pair[side] = run

    pl.semaphore_wait(
        barrier,
        2
        + (chips - 1)
        + (place > 0).astype(jnp.int32)
        + (place < places - 1).astype(jnp.int32),
    )
    swap = pltpu.make_async_remote_copy(
        src_ref=pair.at[side],
        dst_ref=pair.at[side],
        send_sem=pair_send,
        recv_sem=pair_recv,
        device_id=(mate, head),
        device_id_type=MESH,
    )
    swap.start()

    for b in range(blocks):
        query = part(q_ref, b)
        wide = query.astype(F32)
        scale_col = lax.rsqrt(jnp.sum(wide * wide, axis=1, keepdims=True) + 1e-06)
        scores = dot_rows(query, part(k_ref, b))
        scores = jnp.where(row >= col, scores * scale_col * key_rows[b], 0.0)
        seen = dot_wide(scores, writes[b])
        asked = wide * scale_col - seen[:, :width]
        both = dot_wide(asked, prefix[b])
        high, low = halves(both[:, :width])
        rows = slice(b * GROUP, (b + 1) * GROUP)
        eff_high[rows, :] = high
        eff_low[rows, :] = low
        local[rows, :] = both[:, width:] + seen[:, width:]

    swap.wait_recv()
    first = pair[0]
    second = pair[1]
    joined = dot_wide(second[:, :width], first) + beside(nothing, second[:, width:])

    relay = pltpu.make_async_remote_copy(
        src_ref=state_out,
        dst_ref=state_in,
        send_sem=state_send,
        recv_sem=state_recv,
        device_id=(lax.rem(ctx + 2, count), head),
        device_id_type=MESH,
    )

    @pl.when(place == 0)
    def _():
        state_in[...] = nothing
        state_out[...] = joined[:, width:]

    @pl.when(place > 0)
    def _():
        relay.wait_recv()
        state_out[...] = dot_wide(joined[:, :width], state_in[...]) + joined[:, width:]

    @pl.when(place < places - 1)
    def _():
        relay.start()

    start = state_in[...]
    start = jnp.where(
        side == 0, start, dot_wide(first[:, :width], start) + first[:, width:]
    )
    start_high, start_low = halves(start)
    start_all = above(start_high, start_high, start_low)

    size = length // CHUNKS
    gain = gain_ref[...]

    def out_copy(slot, chunk, send_sem, to_head):
        view = gathered.at[slot, pl.ds(chunk * size, size), :]
        return pltpu.make_async_remote_copy(
            src_ref=view,
            dst_ref=view,
            send_sem=send_sem,
            recv_sem=out_recv.at[chunk, slot],
            device_id=(ctx, to_head),
            device_id_type=MESH,
        )

    sent = []
    for chunk in range(CHUNKS):
        rows = slice(chunk * size, (chunk + 1) * size)
        high = eff_high[rows, :]
        result = dot(beside(high, eff_low[rows, :], high), start_all) + local[rows, :]
        power = jnp.mean(result * result, axis=1, keepdims=True)
        gathered[head, rows, :] = (result * lax.rsqrt(power + 1e-06) * gain).astype(BF16)
        for step in range(1, chips):
            copy = out_copy(head, chunk, out_send.at[chunk, step], chip_at(step) * 2 + core)
            copy.start()
            sent.append(copy)
        copy = out_copy(head, chunk, out_send.at[chunk, 0], twin)
        copy.start()
        sent.append(copy)

    def finish(chunk):
        rows = slice(chunk * size, (chunk + 1) * size)
        out_copy(twin, chunk, out_send.at[chunk, 0], twin).wait_recv()
        for step in range(1, chips):
            slot = chip_at(step) * 2 + 1 - core
            out_copy(slot, chunk, forward_send.at[chunk, step], twin).wait_recv()
        joined_rows = beside(*[gathered[slot, rows, :] for slot in range(heads)])
        out_ref[rows, :] = dot(joined_rows, w_ref[...]).astype(BF16)

    for chunk in range(CHUNKS):
        for step in range(1, chips):
            slot = chip_at(step) * 2 + core
            copy = out_copy(slot, chunk, forward_send.at[chunk, step], twin)
            copy.wait_recv()
            copy.start()
            sent.append(copy)
        if chunk > 0:
            finish(chunk - 1)
    finish(CHUNKS - 1)

    for copy in sent:
        copy.wait_send()
    swap.wait_send()

    @pl.when(place < places - 1)
    def _():
        relay.wait_send()


def solution(mesh):
    count, heads = mesh.shape["ctx"], mesh.shape["head"]

    def shards(queries, keys, values, write_rates, norm_gain, w_out):
        length, width = queries.shape
        blocks = length // GROUP
        vmem = pl.BlockSpec(memory_space=pltpu.VMEM)
        wide = (blocks, GROUP, 2 * width)
        return pl.pallas_call(
            functools.partial(kernel, count, heads),
            out_shape=jax.ShapeDtypeStruct((length, w_out.shape[1]), BF16),
            in_specs=[vmem] * 6,
            out_specs=vmem,
            scratch_shapes=[
                pltpu.VMEM((blocks, GROUP, GROUP), F32),
                pltpu.VMEM((blocks, GROUP, GROUP), F32),
                pltpu.VMEM(wide, F32),
                pltpu.VMEM(wide, F32),
                pltpu.VMEM(wide, F32),
                pltpu.VMEM((length, width), BF16),
                pltpu.VMEM((length, width), BF16),
                pltpu.VMEM((length, width), F32),
                pltpu.VMEM((2, GROUP, 2 * width), F32),
                pltpu.VMEM((width, width), F32),
                pltpu.VMEM((width, width), F32),
                pltpu.VMEM((heads, length, width), BF16),
                pltpu.SemaphoreType.DMA,
                pltpu.SemaphoreType.DMA,
                pltpu.SemaphoreType.DMA,
                pltpu.SemaphoreType.DMA,
                pltpu.SemaphoreType.DMA((CHUNKS, heads // 2)),
                pltpu.SemaphoreType.DMA((CHUNKS, heads // 2)),
                pltpu.SemaphoreType.DMA((CHUNKS, heads)),
            ],
            compiler_params=pltpu.CompilerParams(collective_id=0, has_side_effects=True),
        )(queries, keys, values, write_rates, norm_gain.reshape(1, width), w_out)

    return jax.shard_map(
        shards,
        mesh=mesh,
        in_specs=(
            P("ctx", "head"),
            P("ctx", "head"),
            P("ctx", "head"),
            P("head", "ctx"),
            P(),
            P(None, "head"),
        ),
        out_specs=P("ctx", "head"),
        check_vma=False,
    )
```

```python
import functools

import jax
import jax.numpy as jnp
from jax import lax
from jax.experimental import pallas as pl
from jax.experimental.pallas import tpu as pltpu
from jax.sharding import PartitionSpec as P

F32 = jnp.float32
BF16 = jnp.bfloat16
MESH = pl.DeviceIdType.MESH
GROUP = 128
CHUNKS = 4
ROUNDS = 2


def halves(wide):
    high = wide.astype(BF16)
    return high, (wide - high.astype(F32)).astype(BF16)


def dot(left, right):
    return jnp.dot(left, right, preferred_element_type=F32)


def dot_rows(left, right):
    return lax.dot_general(left, right, (((1,), (1,)), ((), ())), preferred_element_type=F32)


def beside(*parts):
    return jnp.concatenate(parts, axis=1)


def above(*parts):
    return jnp.concatenate(parts, axis=0)


def dot_wide(left, right):
    left_high, left_low = halves(left)
    right_high, right_low = halves(right)
    return dot(beside(left_high, left_low, left_high), above(right_high, right_high, right_low))


def dot_rows_wide(left, right):
    left_high, left_low = halves(left)
    right_high, right_low = halves(right)
    return dot_rows(beside(left_high, left_low, left_high), beside(right_high, right_high, right_low))


def kernel(
    count,
    heads,
    q_ref,
    k_ref,
    v_ref,
    rate_ref,
    parts,
    states,
    inverse,
    lower,
    writes,
    pair,
    state_in,
    state_out,
    pair_send,
    pair_recv,
    relay_send,
    relay_recv,
    part_send,
    part_pass,
    part_recv,
    state_send,
    state_pass,
    state_recv,
):
    ctx = lax.axis_index("ctx")
    head = lax.axis_index("head")
    side = lax.rem(ctx, 2)
    place = ctx // 2
    places = count // 2
    mate = ctx + 1 - 2 * side
    core = lax.rem(head, 2)
    chip = head // 2
    chips = heads // 2
    twin = head + 1 - 2 * core
    length, width = q_ref.shape
    blocks = length // GROUP
    chunks = parts.shape[1]
    size = length // chunks

    barrier = pltpu.get_barrier_semaphore()

    def greet(to_ctx, to_head):
        pl.semaphore_signal(barrier, inc=1, device_id=(to_ctx, to_head), device_id_type=MESH)

    def chip_at(step):
        return lax.rem(chip + step, chips)

    greet(mate, head)
    greet(ctx, twin)
    for step in range(1, chips):
        greet(ctx, chip_at(step) * 2 + core)

    @pl.when(place > 0)
    def _():
        greet(ctx - 2, head)

    @pl.when(place < places - 1)
    def _():
        greet(ctx + 2, head)

    row = lax.broadcasted_iota(jnp.int32, (GROUP, GROUP), 0)
    col = lax.broadcasted_iota(jnp.int32, (GROUP, GROUP), 1)
    eye = (row == col).astype(F32)

    rates = above(*[rate_ref[0:1, b * GROUP : (b + 1) * GROUP] for b in range(blocks)])
    rate_cols = rates.T
    key_rows = []
    moves = []

    def part(ref, b):
        return ref[b * GROUP : (b + 1) * GROUP, :]

    for b in range(blocks):
        key = part(k_ref, b)
        wide = key.astype(F32)
        gram = dot_rows(key, key)
        scale_col = lax.rsqrt(jnp.sum(wide * wide, axis=1, keepdims=True) + 1e-06)
        scale_row = lax.rsqrt(jnp.sum(gram * eye, axis=0, keepdims=True) + 1e-06)
        key_rows.append(scale_row)
        strict = jnp.where(
            row > col, gram * (rate_cols[:, b : b + 1] * scale_col) * scale_row, 0.0
        )
        lower[b] = strict
        near = (row // 2 == col // 2) & (row != col)
        inverse[b] = eye - jnp.where(near, strict, 0.0)

    span = 2
    while span < GROUP:
        corner = (row // (2 * span) == col // (2 * span)) & (row // span != col // span)
        for b in range(blocks):
            held = inverse[b]
            inverse[b] = held - dot_wide(
                held, dot_wide(jnp.where(corner, lower[b], 0.0), held)
            )
        span *= 2

    for b in range(blocks):
        key = part(k_ref, b)
        value = part(v_ref, b)
        wide = key.astype(F32)
        scale_col = lax.rsqrt(jnp.sum(wide * wide, axis=1, keepdims=True) + 1e-06)
        spread = inverse[b] * rates[b : b + 1, :]
        key_high, key_low = halves(spread * key_rows[b])
        value_high, value_low = halves(spread)
        written = beside(
            dot(beside(key_high, key_low), above(key, key)),
            dot(beside(value_high, value_low), above(value, value)),
        )
        writes[b] = written
        high, low = halves(written * scale_col)
        turned = key.T
        moved = dot(beside(turned, turned), above(high, low))
        moves.append(beside(eye - moved[:, :width], moved[:, width:]))

    nothing = jnp.zeros((GROUP, width), F32)

    def after(later, earlier):
        return dot_wide(later[:, :width], earlier) + beside(nothing, later[:, width:])

    ranges = {(b, b + 1): moves[b] for b in range(blocks)}
    reach = 1
    while reach < blocks:
        for b in range(0, blocks, 2 * reach):
            middle, end = min(b + reach, blocks), min(b + 2 * reach, blocks)
            if middle < end:
                ranges[b, end] = after(ranges[middle, end], ranges[b, middle])
        reach *= 2
    pair[side] = ranges[0, blocks]

    pl.semaphore_wait(
        barrier,
        2
        + (chips - 1)
        + (place > 0).astype(jnp.int32)
        + (place < places - 1).astype(jnp.int32),
    )
    swap = pltpu.make_async_remote_copy(
        src_ref=pair.at[side],
        dst_ref=pair.at[side],
        send_sem=pair_send,
        recv_sem=pair_recv,
        device_id=(mate, head),
        device_id_type=MESH,
    )
    swap.start()

    for b in range(1, blocks):
        if (0, b) not in ranges:
            low = b & -b
            ranges[0, b] = after(ranges[b - low, b], ranges[0, b - low])

    def part_copy(slot, chunk, send_sem, to_head):
        return pltpu.make_async_remote_copy(
            src_ref=parts.at[slot, chunk],
            dst_ref=parts.at[slot, chunk],
            send_sem=send_sem,
            recv_sem=part_recv.at[chunk, slot],
            device_id=(ctx, to_head),
            device_id_type=MESH,
        )

    def state_copy(slot, send_sem, to_head):
        return pltpu.make_async_remote_copy(
            src_ref=states.at[slot],
            dst_ref=states.at[slot],
            send_sem=send_sem,
            recv_sem=state_recv.at[slot],
            device_id=(ctx, to_head),
            device_id_type=MESH,
        )

    sent = []
    for b in range(blocks):
        query = part(q_ref, b)
        wide = query.astype(F32)
        scale_col = lax.rsqrt(jnp.sum(wide * wide, axis=1, keepdims=True) + 1e-06)
        scores = dot_rows(query, part(k_ref, b))
        scores = jnp.where(row >= col, scores * scale_col * key_rows[b], 0.0)
        seen = dot_wide(scores, writes[b])
        asked = wide * scale_col - seen[:, :width]
        if b == 0:
            both = beside(asked, nothing)
        else:
            both = dot_wide(asked, ranges[0, b])
        chunk, at = divmod(b * GROUP, size)
        parts[head, chunk, 0, at : at + GROUP, :] = both[:, :width].astype(BF16)
        parts[head, chunk, 1, at : at + GROUP, :] = (both[:, width:] + seen[:, width:]).astype(BF16)
        if at + GROUP == size:
            for step in range(1, chips):
                copy = part_copy(head, chunk, part_send.at[chunk, step], chip_at(step) * 2 + core)
                copy.start()
                sent.append(copy)
            copy = part_copy(head, chunk, part_send.at[chunk, 0], twin)
            copy.start()
            sent.append(copy)

    swap.wait_recv()
    first = pair[0]
    second = pair[1]
    joined = after(second, first)
    joined_map = joined[:, :width]
    joined_add = joined[:, width:].T

    rounds = state_in.shape[0]
    tall = width // rounds

    def relay(turn):
        return pltpu.make_async_remote_copy(
            src_ref=state_out.at[turn],
            dst_ref=state_in.at[turn],
            send_sem=relay_send.at[turn],
            recv_sem=relay_recv.at[turn],
            device_id=(lax.rem(ctx + 2, count), head),
            device_id_type=MESH,
        )

    for turn in range(rounds):
        rows = slice(turn * tall, (turn + 1) * tall)

        @pl.when(place == 0)
        def _():
            state_in[turn] = jnp.zeros((tall, width), F32)
            state_out[turn] = joined_add[rows, :]

        @pl.when(place > 0)
        def _():
            relay(turn).wait_recv()

            @pl.when(place < places - 1)
            def _():
                state_out[turn] = dot_rows_wide(state_in[turn], joined_map) + joined_add[rows, :]

        @pl.when(place < places - 1)
        def _():
            relay(turn).start()

    start = state_in[...].reshape(width, width)
    states[head] = jnp.where(
        side == 0, start, dot_rows_wide(start, first[:, :width]) + first[:, width:].T
    )
    for step in range(1, chips):
        copy = state_copy(head, state_send.at[step], chip_at(step) * 2 + core)
        copy.start()
        sent.append(copy)
    copy = state_copy(head, state_send.at[0], twin)
    copy.start()
    sent.append(copy)

    for chunk in range(chunks):
        for step in range(1, chips):
            slot = chip_at(step) * 2 + core
            copy = part_copy(slot, chunk, part_pass.at[chunk, step], twin)
            copy.wait_recv()
            copy.start()
            sent.append(copy)
    for step in range(1, chips):
        slot = chip_at(step) * 2 + core
        copy = state_copy(slot, state_pass.at[step], twin)
        copy.wait_recv()
        copy.start()
        sent.append(copy)

    for chunk in range(chunks):
        part_copy(twin, chunk, part_send.at[chunk, 0], twin).wait_recv()
        for step in range(1, chips):
            slot = chip_at(step) * 2 + 1 - core
            part_copy(slot, chunk, part_pass.at[chunk, step], twin).wait_recv()
    state_copy(twin, state_send.at[0], twin).wait_recv()
    for step in range(1, chips):
        slot = chip_at(step) * 2 + 1 - core
        state_copy(slot, state_pass.at[step], twin).wait_recv()

    for copy in sent:
        copy.wait_send()
    swap.wait_send()

    @pl.when(place < places - 1)
    def _():
        for turn in range(rounds):
            relay(turn).wait_send()


def finish(parts, states, gain_ref, w_ref, out_ref):
    heads = parts.shape[0]
    gain = gain_ref[...]
    rows = []
    for slot in range(heads):
        high, low = halves(states[slot])
        asked = parts[slot, 0, 0]
        result = dot_rows(beside(asked, asked), beside(high, low)) + parts[slot, 0, 1].astype(F32)
        power = jnp.mean(result * result, axis=1, keepdims=True)
        rows.append((result * lax.rsqrt(power + 1e-06) * gain).astype(BF16))
    out_ref[...] = dot(beside(*rows), w_ref[...]).astype(BF16)


def solution(mesh):
    count, heads = mesh.shape["ctx"], mesh.shape["head"]

    def shards(queries, keys, values, write_rates, norm_gain, w_out):
        length, width = queries.shape
        blocks = length // GROUP
        size = length // CHUNKS
        columns = w_out.shape[1]
        vmem = pl.BlockSpec(memory_space=pltpu.VMEM)
        parts, states = pl.pallas_call(
            functools.partial(kernel, count, heads),
            out_shape=(
                jax.ShapeDtypeStruct((heads, CHUNKS, 2, size, width), BF16),
                jax.ShapeDtypeStruct((heads, width, width), F32),
            ),
            in_specs=[vmem] * 4,
            out_specs=(vmem, vmem),
            scratch_shapes=[
                pltpu.VMEM((blocks, GROUP, GROUP), F32),
                pltpu.VMEM((blocks, GROUP, GROUP), F32),
                pltpu.VMEM((blocks, GROUP, 2 * width), F32),
                pltpu.VMEM((2, GROUP, 2 * width), F32),
                pltpu.VMEM((ROUNDS, width // ROUNDS, width), F32),
                pltpu.VMEM((ROUNDS, width // ROUNDS, width), F32),
                pltpu.SemaphoreType.DMA,
                pltpu.SemaphoreType.DMA,
                pltpu.SemaphoreType.DMA((ROUNDS,)),
                pltpu.SemaphoreType.DMA((ROUNDS,)),
                pltpu.SemaphoreType.DMA((CHUNKS, heads // 2)),
                pltpu.SemaphoreType.DMA((CHUNKS, heads // 2)),
                pltpu.SemaphoreType.DMA((CHUNKS, heads)),
                pltpu.SemaphoreType.DMA((heads // 2,)),
                pltpu.SemaphoreType.DMA((heads // 2,)),
                pltpu.SemaphoreType.DMA((heads,)),
            ],
            compiler_params=pltpu.CompilerParams(
                collective_id=0, has_side_effects=True, vmem_limit_bytes=24 << 20
            ),
        )(queries, keys, values, write_rates)
        return pl.pallas_call(
            finish,
            out_shape=jax.ShapeDtypeStruct((length, columns), BF16),
            grid=(CHUNKS,),
            in_specs=[
                pl.BlockSpec((heads, 1, 2, size, width), lambda i: (0, i, 0, 0, 0)),
                pl.BlockSpec((heads, width, width), lambda i: (0, 0, 0)),
                pl.BlockSpec((1, width), lambda i: (0, 0)),
                pl.BlockSpec(w_out.shape, lambda i: (0, 0)),
            ],
            out_specs=pl.BlockSpec((size, columns), lambda i: (i, 0)),
            compiler_params=pltpu.CompilerParams(vmem_limit_bytes=24 << 20),
        )(parts, states, norm_gain.reshape(1, width), w_out)

    return jax.shard_map(
        shards,
        mesh=mesh,
        in_specs=(
            P("ctx", "head"),
            P("ctx", "head"),
            P("ctx", "head"),
            P("head", "ctx"),
            P(),
            P(None, "head"),
        ),
        out_specs=P("ctx", "head"),
        check_vma=False,
    )
```

```python
import functools

import jax
import jax.numpy as jnp
from jax import lax
from jax.experimental import pallas as pl
from jax.experimental.pallas import tpu as pltpu
from jax.sharding import PartitionSpec as P

F32 = jnp.float32
BF16 = jnp.bfloat16
MESH = pl.DeviceIdType.MESH
GROUP = 128
CHUNKS = 4
ROUNDS = 2


def halves(wide):
    high = wide.astype(BF16)
    return high, (wide - high.astype(F32)).astype(BF16)


def dot(left, right):
    return jnp.dot(left, right, preferred_element_type=F32)


def dot_rows(left, right):
    return lax.dot_general(left, right, (((1,), (1,)), ((), ())), preferred_element_type=F32)


def beside(*parts):
    return jnp.concatenate(parts, axis=1)


def above(*parts):
    return jnp.concatenate(parts, axis=0)


def dot_wide(left, right):
    left_high, left_low = halves(left)
    right_high, right_low = halves(right)
    return dot(beside(left_high, left_low, left_high), above(right_high, right_high, right_low))


def dot_rows_wide(left, right):
    left_high, left_low = halves(left)
    right_high, right_low = halves(right)
    return dot_rows(beside(left_high, left_low, left_high), beside(right_high, right_high, right_low))


def kernel(
    count,
    heads,
    q_hbm,
    k_hbm,
    v_hbm,
    rate_hbm,
    gain_hbm,
    w_hbm,
    parts,
    states,
    gain_out,
    w_out,
    q_ref,
    k_ref,
    v_ref,
    rate_ref,
    inverse,
    coarse,
    lower,
    writes,
    pair,
    state_in,
    state_out,
    load_sem,
    pair_send,
    pair_recv,
    relay_send,
    relay_recv,
    part_send,
    part_pass,
    part_recv,
    state_send,
    state_pass,
    state_recv,
):
    ctx = lax.axis_index("ctx")
    head = lax.axis_index("head")
    side = lax.rem(ctx, 2)
    place = ctx // 2
    places = count // 2
    mate = ctx + 1 - 2 * side
    core = lax.rem(head, 2)
    chip = head // 2
    chips = heads // 2
    twin = head + 1 - 2 * core
    length, width = q_ref.shape
    blocks = length // GROUP
    chunks = parts.shape[1]
    size = length // chunks

    loads = [
        pltpu.make_async_copy(source, target, load_sem.at[at])
        for at, (source, target) in enumerate(
            (
                (k_hbm, k_ref),
                (rate_hbm, rate_ref),
                (v_hbm, v_ref),
                (q_hbm, q_ref),
                (w_hbm, w_out),
                (gain_hbm, gain_out),
            )
        )
    ]
    for load in loads:
        load.start()
    barrier = pltpu.get_barrier_semaphore()

    def greet(to_ctx, to_head):
        pl.semaphore_signal(barrier, inc=1, device_id=(to_ctx, to_head), device_id_type=MESH)

    def chip_at(step):
        return lax.rem(chip + step, chips)

    greet(mate, head)
    greet(ctx, twin)
    for step in range(1, chips):
        greet(ctx, chip_at(step) * 2 + core)

    @pl.when(place > 0)
    def _():
        greet(ctx - 2, head)

    @pl.when(place < places - 1)
    def _():
        greet(ctx + 2, head)

    row = lax.broadcasted_iota(jnp.int32, (GROUP, GROUP), 0)
    col = lax.broadcasted_iota(jnp.int32, (GROUP, GROUP), 1)
    eye = (row == col).astype(F32)

    loads[0].wait()
    loads[1].wait()
    rates = above(*[rate_ref[0:1, b * GROUP : (b + 1) * GROUP] for b in range(blocks)])
    rate_cols = rates.T
    key_rows = []
    moves = []

    def part(ref, b):
        return ref[b * GROUP : (b + 1) * GROUP, :]

    for b in range(blocks):
        key = part(k_ref, b)
        wide = key.astype(F32)
        gram = dot_rows(key, key)
        scale_col = lax.rsqrt(jnp.sum(wide * wide, axis=1, keepdims=True) + 1e-06)
        scale_row = lax.rsqrt(jnp.sum(gram * eye, axis=0, keepdims=True) + 1e-06)
        key_rows.append(scale_row)
        strict = jnp.where(
            row > col, gram * (rate_cols[:, b : b + 1] * scale_col) * scale_row, 0.0
        )
        lower[b] = strict
        coarse[b] = strict.astype(BF16)
        near = (row // 2 == col // 2) & (row != col)
        inverse[b] = (eye - jnp.where(near, strict, 0.0)).astype(BF16)

    span = 2
    while span < GROUP:
        corner = (
            ((row // (2 * span) == col // (2 * span)) & (row // span != col // span))
            .astype(F32)
            .astype(BF16)
        )
        spots = [slice(at, at + span) for at in range(span, GROUP, 2 * span)]
        if span < 16:
            spots = [slice(0, GROUP)]
        for b in range(blocks):
            held = inverse[b]
            rows = above(*[held[spot, :] for spot in spots])
            change = dot(dot(rows, coarse[b] * corner).astype(BF16), held).astype(BF16)
            rows = rows - change
            at = 0
            for spot in spots:
                tall = spot.stop - spot.start
                inverse[b, spot, :] = rows[at : at + tall, :]
                at += tall
        span *= 2

    loads[2].wait()
    for b in range(blocks):
        key = part(k_ref, b)
        value = part(v_ref, b)
        wide = key.astype(F32)
        scale_col = lax.rsqrt(jnp.sum(wide * wide, axis=1, keepdims=True) + 1e-06)
        held = inverse[b]
        high, low = halves(lower[b])
        miss = eye - held.astype(F32) - dot(beside(high, low), above(held, held))
        rough = miss.astype(BF16)
        miss = miss + dot(rough, rough)
        exact = held.astype(F32) + dot(held, miss.astype(BF16))
        spread = exact * rates[b : b + 1, :]
        key_high, key_low = halves(spread * key_rows[b])
        value_high, value_low = halves(spread)
        written = beside(
            dot(beside(key_high, key_low), above(key, key)),
            dot(beside(value_high, value_low), above(value, value)),
        )
        writes[b] = written
        high, low = halves(written * scale_col)
        turned = key.T
        moved = dot(beside(turned, turned), above(high, low))
        moves.append(beside(eye - moved[:, :width], moved[:, width:]))

    nothing = jnp.zeros((GROUP, width), F32)

    def after(later, earlier):
        return dot_wide(later[:, :width], earlier) + beside(nothing, later[:, width:])

    ranges = {(b, b + 1): moves[b] for b in range(blocks)}
    reach = 1
    while reach < blocks:
        for b in range(0, blocks, 2 * reach):
            middle, end = min(b + reach, blocks), min(b + 2 * reach, blocks)
            if middle < end:
                ranges[b, end] = after(ranges[middle, end], ranges[b, middle])
        reach *= 2
    pair[side] = ranges[0, blocks]

    pl.semaphore_wait(
        barrier,
        2
        + (chips - 1)
        + (place > 0).astype(jnp.int32)
        + (place < places - 1).astype(jnp.int32),
    )
    swap = pltpu.make_async_remote_copy(
        src_ref=pair.at[side],
        dst_ref=pair.at[side],
        send_sem=pair_send,
        recv_sem=pair_recv,
        device_id=(mate, head),
        device_id_type=MESH,
    )
    swap.start()

    loads[3].wait()
    for b in range(1, blocks):
        if (0, b) not in ranges:
            low = b & -b
            ranges[0, b] = after(ranges[b - low, b], ranges[0, b - low])

    def part_copy(slot, chunk, send_sem, to_head):
        return pltpu.make_async_remote_copy(
            src_ref=parts.at[slot, chunk],
            dst_ref=parts.at[slot, chunk],
            send_sem=send_sem,
            recv_sem=part_recv.at[chunk, slot],
            device_id=(ctx, to_head),
            device_id_type=MESH,
        )

    def state_copy(slot, send_sem, to_head):
        return pltpu.make_async_remote_copy(
            src_ref=states.at[slot],
            dst_ref=states.at[slot],
            send_sem=send_sem,
            recv_sem=state_recv.at[slot],
            device_id=(ctx, to_head),
            device_id_type=MESH,
        )

    sent = []
    for b in range(blocks):
        query = part(q_ref, b)
        wide = query.astype(F32)
        scale_col = lax.rsqrt(jnp.sum(wide * wide, axis=1, keepdims=True) + 1e-06)
        scores = dot_rows(query, part(k_ref, b))
        scores = jnp.where(row >= col, scores * scale_col * key_rows[b], 0.0)
        seen = dot_wide(scores, writes[b])
        asked = wide * scale_col - seen[:, :width]
        if b == 0:
            both = beside(asked, nothing)
        else:
            both = dot_wide(asked, ranges[0, b])
        chunk, at = divmod(b * GROUP, size)
        parts[head, chunk, 0, at : at + GROUP, :] = both[:, :width].astype(BF16)
        parts[head, chunk, 1, at : at + GROUP, :] = (both[:, width:] + seen[:, width:]).astype(BF16)
        if at + GROUP == size:
            for step in range(1, chips):
                copy = part_copy(head, chunk, part_send.at[chunk, step], chip_at(step) * 2 + core)
                copy.start()
                sent.append(copy)
            copy = part_copy(head, chunk, part_send.at[chunk, 0], twin)
            copy.start()
            sent.append(copy)

    swap.wait_recv()
    first = pair[0]
    second = pair[1]
    joined = after(second, first)
    joined_map = joined[:, :width]
    joined_add = joined[:, width:].T

    rounds = state_in.shape[0]
    tall = width // rounds

    def relay(turn):
        return pltpu.make_async_remote_copy(
            src_ref=state_out.at[turn],
            dst_ref=state_in.at[turn],
            send_sem=relay_send.at[turn],
            recv_sem=relay_recv.at[turn],
            device_id=(lax.rem(ctx + 2, count), head),
            device_id_type=MESH,
        )

    for turn in range(rounds):
        rows = slice(turn * tall, (turn + 1) * tall)

        @pl.when(place == 0)
        def _():
            state_in[turn] = jnp.zeros((tall, width), F32)
            state_out[turn] = joined_add[rows, :]

        @pl.when(place > 0)
        def _():
            relay(turn).wait_recv()

            @pl.when(place < places - 1)
            def _():
                state_out[turn] = dot_rows_wide(state_in[turn], joined_map) + joined_add[rows, :]

        @pl.when(place < places - 1)
        def _():
            relay(turn).start()

    start = state_in[...].reshape(width, width)
    states[head] = jnp.where(
        side == 0, start, dot_rows_wide(start, first[:, :width]) + first[:, width:].T
    )
    for step in range(1, chips):
        copy = state_copy(head, state_send.at[step], chip_at(step) * 2 + core)
        copy.start()
        sent.append(copy)
    copy = state_copy(head, state_send.at[0], twin)
    copy.start()
    sent.append(copy)

    for chunk in range(chunks):
        for step in range(1, chips):
            slot = chip_at(step) * 2 + core
            copy = part_copy(slot, chunk, part_pass.at[chunk, step], twin)
            copy.wait_recv()
            copy.start()
            sent.append(copy)
    for step in range(1, chips):
        slot = chip_at(step) * 2 + core
        copy = state_copy(slot, state_pass.at[step], twin)
        copy.wait_recv()
        copy.start()
        sent.append(copy)

    for chunk in range(chunks):
        part_copy(twin, chunk, part_send.at[chunk, 0], twin).wait_recv()
        for step in range(1, chips):
            slot = chip_at(step) * 2 + 1 - core
            part_copy(slot, chunk, part_pass.at[chunk, step], twin).wait_recv()
    state_copy(twin, state_send.at[0], twin).wait_recv()
    for step in range(1, chips):
        slot = chip_at(step) * 2 + 1 - core
        state_copy(slot, state_pass.at[step], twin).wait_recv()

    for copy in sent:
        copy.wait_send()
    swap.wait_send()
    loads[4].wait()
    loads[5].wait()

    @pl.when(place < places - 1)
    def _():
        for turn in range(rounds):
            relay(turn).wait_send()


def finish(parts, states, gain_ref, w_ref, out_ref, staged, sems):
    heads, chunks = parts.shape[:2]
    size, width = parts.shape[3:]
    gain = gain_ref[...]
    share = jnp.full((2 * width, width), 1.0 / width, BF16)
    starts = [beside(*halves(states[slot])) for slot in range(heads)]
    copies = []
    for chunk in range(chunks):
        rows = []
        for slot in range(heads):
            asked = parts[slot, chunk, 0]
            result = dot_rows(beside(asked, asked), starts[slot])
            result = result + parts[slot, chunk, 1].astype(F32)
            power = dot(beside(*halves(result * result)), share)
            rows.append((result * lax.rsqrt(power + 1e-06) * gain).astype(BF16))
        staged[chunk] = dot(beside(*rows), w_ref[...]).astype(BF16)
        copy = pltpu.make_async_copy(
            staged.at[chunk], out_ref.at[pl.ds(chunk * size, size), :], sems.at[chunk]
        )
        copy.start()
        copies.append(copy)
    for copy in copies:
        copy.wait()


def solution(mesh):
    count, heads = mesh.shape["ctx"], mesh.shape["head"]

    def shards(queries, keys, values, write_rates, norm_gain, w_out):
        length, width = queries.shape
        blocks = length // GROUP
        size = length // CHUNKS
        columns = w_out.shape[1]
        vmem = pl.BlockSpec(memory_space=pltpu.VMEM)
        hbm = pl.BlockSpec(memory_space=pltpu.MemorySpace.HBM)
        parts, states, gain, weights = pl.pallas_call(
            functools.partial(kernel, count, heads),
            out_shape=(
                jax.ShapeDtypeStruct((heads, CHUNKS, 2, size, width), BF16),
                jax.ShapeDtypeStruct((heads, width, width), F32),
                jax.ShapeDtypeStruct((1, width), F32),
                jax.ShapeDtypeStruct(w_out.shape, BF16),
            ),
            in_specs=[hbm] * 6,
            out_specs=(vmem,) * 4,
            scratch_shapes=[
                pltpu.VMEM((length, width), BF16),
                pltpu.VMEM((length, width), BF16),
                pltpu.VMEM((length, width), BF16),
                pltpu.VMEM((1, length), F32),
                pltpu.VMEM((blocks, GROUP, GROUP), BF16),
                pltpu.VMEM((blocks, GROUP, GROUP), BF16),
                pltpu.VMEM((blocks, GROUP, GROUP), F32),
                pltpu.VMEM((blocks, GROUP, 2 * width), F32),
                pltpu.VMEM((2, GROUP, 2 * width), F32),
                pltpu.VMEM((ROUNDS, width // ROUNDS, width), F32),
                pltpu.VMEM((ROUNDS, width // ROUNDS, width), F32),
                pltpu.SemaphoreType.DMA((6,)),
                pltpu.SemaphoreType.DMA,
                pltpu.SemaphoreType.DMA,
                pltpu.SemaphoreType.DMA((ROUNDS,)),
                pltpu.SemaphoreType.DMA((ROUNDS,)),
                pltpu.SemaphoreType.DMA((CHUNKS, heads // 2)),
                pltpu.SemaphoreType.DMA((CHUNKS, heads // 2)),
                pltpu.SemaphoreType.DMA((CHUNKS, heads)),
                pltpu.SemaphoreType.DMA((heads // 2,)),
                pltpu.SemaphoreType.DMA((heads // 2,)),
                pltpu.SemaphoreType.DMA((heads,)),
            ],
            compiler_params=pltpu.CompilerParams(
                collective_id=0, has_side_effects=True, vmem_limit_bytes=24 << 20
            ),
        )(*[
            pltpu.with_memory_space_constraint(given, pltpu.MemorySpace.HBM)
            for given in (queries, keys, values, write_rates, norm_gain.reshape(1, width), w_out)
        ])
        return pl.pallas_call(
            finish,
            out_shape=jax.ShapeDtypeStruct((length, columns), BF16),
            in_specs=[vmem] * 4,
            out_specs=pl.BlockSpec(memory_space=pltpu.MemorySpace.HBM),
            scratch_shapes=[
                pltpu.VMEM((CHUNKS, size, columns), BF16),
                pltpu.SemaphoreType.DMA((CHUNKS,)),
            ],
            compiler_params=pltpu.CompilerParams(vmem_limit_bytes=24 << 20),
        )(parts, states, gain, weights)

    return jax.shard_map(
        shards,
        mesh=mesh,
        in_specs=(
            P("ctx", "head"),
            P("ctx", "head"),
            P("ctx", "head"),
            P("head", "ctx"),
            P(),
            P(None, "head"),
        ),
        out_specs=P("ctx", "head"),
        check_vma=False,
    )
```

```python
import functools

import jax
import jax.numpy as jnp
from jax import lax
from jax.experimental import pallas as pl
from jax.experimental.pallas import tpu as pltpu
from jax.sharding import PartitionSpec as P

F32 = jnp.float32
BF16 = jnp.bfloat16
MESH = pl.DeviceIdType.MESH
GROUP = 128
CHUNKS = 4
ROUNDS = 2


def halves(wide):
    high = wide.astype(BF16)
    return high, (wide - high.astype(F32)).astype(BF16)


def dot(left, right):
    return jnp.dot(left, right, preferred_element_type=F32)


def dot_rows(left, right):
    return lax.dot_general(left, right, (((1,), (1,)), ((), ())), preferred_element_type=F32)


def beside(*parts):
    return jnp.concatenate(parts, axis=1)


def above(*parts):
    return jnp.concatenate(parts, axis=0)


def dot_wide(left, right):
    left_high, left_low = halves(left)
    right_high, right_low = halves(right)
    return dot(beside(left_high, left_low, left_high), above(right_high, right_high, right_low))


def dot_rows_wide(left, right):
    left_high, left_low = halves(left)
    right_high, right_low = halves(right)
    return dot_rows(beside(left_high, left_low, left_high), beside(right_high, right_high, right_low))


def settled(parts, slot, chunk, start, gain, share):
    asked = parts[slot, chunk, 0]
    result = dot_rows(beside(asked, asked), start) + parts[slot, chunk, 1].astype(F32)
    power = dot(beside(*halves(result * result)), share)
    return (result * lax.rsqrt(power + 1e-06) * gain).astype(BF16)


def kernel(
    count,
    heads,
    q_hbm,
    k_hbm,
    v_hbm,
    rate_hbm,
    gain_hbm,
    w_hbm,
    parts,
    states,
    gain_out,
    w_out,
    done,
    q_ref,
    k_ref,
    v_ref,
    rate_ref,
    inverse,
    coarse,
    lower,
    writes,
    mine,
    pair,
    state_in,
    state_out,
    load_sem,
    pair_send,
    pair_recv,
    relay_send,
    relay_recv,
    part_send,
    part_pass,
    part_recv,
    state_send,
    state_pass,
    state_recv,
):
    ctx = lax.axis_index("ctx")
    head = lax.axis_index("head")
    side = lax.rem(ctx, 2)
    place = ctx // 2
    places = count // 2
    mate = ctx + 1 - 2 * side
    core = lax.rem(head, 2)
    chip = head // 2
    chips = heads // 2
    twin = head + 1 - 2 * core
    length, width = q_ref.shape
    blocks = length // GROUP
    chunks = parts.shape[1]
    size = length // chunks

    loads = [
        pltpu.make_async_copy(source, target, load_sem.at[at])
        for at, (source, target) in enumerate(
            (
                (k_hbm, k_ref),
                (rate_hbm, rate_ref),
                (v_hbm, v_ref),
                (q_hbm, q_ref),
                (w_hbm, w_out),
                (gain_hbm, gain_out),
            )
        )
    ]
    for load in loads:
        load.start()
    barrier = pltpu.get_barrier_semaphore()

    def greet(to_ctx, to_head):
        pl.semaphore_signal(barrier, inc=1, device_id=(to_ctx, to_head), device_id_type=MESH)

    def chip_at(step):
        return lax.rem(chip + step, chips)

    greet(mate, head)
    greet(ctx, twin)
    for step in range(1, chips):
        greet(ctx, chip_at(step) * 2 + core)

    @pl.when(place > 0)
    def _():
        greet(ctx - 2, head)

    @pl.when(place < places - 1)
    def _():
        greet(ctx + 2, head)

    row = lax.broadcasted_iota(jnp.int32, (GROUP, GROUP), 0)
    col = lax.broadcasted_iota(jnp.int32, (GROUP, GROUP), 1)
    eye = (row == col).astype(F32)

    loads[0].wait()
    loads[1].wait()
    rates = above(*[rate_ref[0:1, b * GROUP : (b + 1) * GROUP] for b in range(blocks)])
    rate_cols = rates.T
    key_rows = []
    moves = []

    def part(ref, b):
        return ref[b * GROUP : (b + 1) * GROUP, :]

    for b in range(blocks):
        key = part(k_ref, b)
        wide = key.astype(F32)
        gram = dot_rows(key, key)
        scale_col = lax.rsqrt(jnp.sum(wide * wide, axis=1, keepdims=True) + 1e-06)
        scale_row = lax.rsqrt(jnp.sum(gram * eye, axis=0, keepdims=True) + 1e-06)
        key_rows.append(scale_row)
        strict = jnp.where(
            row > col, gram * (rate_cols[:, b : b + 1] * scale_col) * scale_row, 0.0
        )
        lower[b] = strict
        coarse[b] = strict.astype(BF16)
        near = (row // 2 == col // 2) & (row != col)
        inverse[b] = (eye - jnp.where(near, strict, 0.0)).astype(BF16)

    span = 2
    while span < GROUP:
        corner = (
            ((row // (2 * span) == col // (2 * span)) & (row // span != col // span))
            .astype(F32)
            .astype(BF16)
        )
        spots = [slice(at, at + span) for at in range(span, GROUP, 2 * span)]
        if span < 16:
            spots = [slice(0, GROUP)]
        for b in range(blocks):
            held = inverse[b]
            rows = above(*[held[spot, :] for spot in spots])
            change = dot(dot(rows, coarse[b] * corner).astype(BF16), held).astype(BF16)
            rows = rows - change
            at = 0
            for spot in spots:
                tall = spot.stop - spot.start
                inverse[b, spot, :] = rows[at : at + tall, :]
                at += tall
        span *= 2

    loads[2].wait()
    for b in range(blocks):
        key = part(k_ref, b)
        value = part(v_ref, b)
        wide = key.astype(F32)
        scale_col = lax.rsqrt(jnp.sum(wide * wide, axis=1, keepdims=True) + 1e-06)
        held = inverse[b]
        high, low = halves(lower[b])
        miss = eye - held.astype(F32) - dot(beside(high, low), above(held, held))
        rough = miss.astype(BF16)
        miss = miss + dot(rough, rough)
        exact = held.astype(F32) + dot(held, miss.astype(BF16))
        spread = exact * rates[b : b + 1, :]
        key_high, key_low = halves(spread * key_rows[b])
        value_high, value_low = halves(spread)
        written = beside(
            dot(beside(key_high, key_low), above(key, key)),
            dot(beside(value_high, value_low), above(value, value)),
        )
        writes[b] = written
        high, low = halves(written * scale_col)
        turned = key.T
        moved = dot(beside(turned, turned), above(high, low))
        moves.append(beside(eye - moved[:, :width], moved[:, width:]))

    nothing = jnp.zeros((GROUP, width), F32)

    def after(later, earlier):
        return dot_wide(later[:, :width], earlier) + beside(nothing, later[:, width:])

    ranges = {(b, b + 1): moves[b] for b in range(blocks)}
    reach = 1
    while reach < blocks:
        for b in range(0, blocks, 2 * reach):
            middle, end = min(b + reach, blocks), min(b + 2 * reach, blocks)
            if middle < end:
                ranges[b, end] = after(ranges[middle, end], ranges[b, middle])
        reach *= 2
    pair[side] = ranges[0, blocks]

    pl.semaphore_wait(
        barrier,
        2
        + (chips - 1)
        + (place > 0).astype(jnp.int32)
        + (place < places - 1).astype(jnp.int32),
    )
    swap = pltpu.make_async_remote_copy(
        src_ref=pair.at[side],
        dst_ref=pair.at[side],
        send_sem=pair_send,
        recv_sem=pair_recv,
        device_id=(mate, head),
        device_id_type=MESH,
    )
    swap.start()

    loads[3].wait()
    for b in range(1, blocks):
        if (0, b) not in ranges:
            low = b & -b
            ranges[0, b] = after(ranges[b - low, b], ranges[0, b - low])

    def part_copy(slot, chunk, send_sem, to_head):
        return pltpu.make_async_remote_copy(
            src_ref=parts.at[slot, chunk],
            dst_ref=parts.at[slot, chunk],
            send_sem=send_sem,
            recv_sem=part_recv.at[chunk, slot],
            device_id=(ctx, to_head),
            device_id_type=MESH,
        )

    def state_copy(slot, send_sem, to_head):
        return pltpu.make_async_remote_copy(
            src_ref=states.at[slot],
            dst_ref=states.at[slot],
            send_sem=send_sem,
            recv_sem=state_recv.at[slot],
            device_id=(ctx, to_head),
            device_id_type=MESH,
        )

    sent = []
    for b in range(blocks):
        query = part(q_ref, b)
        wide = query.astype(F32)
        scale_col = lax.rsqrt(jnp.sum(wide * wide, axis=1, keepdims=True) + 1e-06)
        scores = dot_rows(query, part(k_ref, b))
        scores = jnp.where(row >= col, scores * scale_col * key_rows[b], 0.0)
        seen = dot_wide(scores, writes[b])
        asked = wide * scale_col - seen[:, :width]
        if b == 0:
            both = beside(asked, nothing)
        else:
            both = dot_wide(asked, ranges[0, b])
        chunk, at = divmod(b * GROUP, size)
        parts[head, chunk, 0, at : at + GROUP, :] = both[:, :width].astype(BF16)
        parts[head, chunk, 1, at : at + GROUP, :] = (both[:, width:] + seen[:, width:]).astype(BF16)
        if at + GROUP == size:
            for step in range(1, chips):
                copy = part_copy(head, chunk, part_send.at[chunk, step], chip_at(step) * 2 + core)
                copy.start()
                sent.append(copy)
            copy = part_copy(head, chunk, part_send.at[chunk, 0], twin)
            copy.start()
            sent.append(copy)

    swap.wait_recv()
    first = pair[0]
    second = pair[1]
    joined = after(second, first)
    joined_map = joined[:, :width]
    joined_add = joined[:, width:].T

    rounds = state_in.shape[0]
    tall = width // rounds

    def relay(turn):
        return pltpu.make_async_remote_copy(
            src_ref=state_out.at[turn],
            dst_ref=state_in.at[turn],
            send_sem=relay_send.at[turn],
            recv_sem=relay_recv.at[turn],
            device_id=(lax.rem(ctx + 2, count), head),
            device_id_type=MESH,
        )

    for turn in range(rounds):
        rows = slice(turn * tall, (turn + 1) * tall)

        @pl.when(place == 0)
        def _():
            state_in[turn] = jnp.zeros((tall, width), F32)
            state_out[turn] = joined_add[rows, :]

        @pl.when(place > 0)
        def _():
            relay(turn).wait_recv()

            @pl.when(place < places - 1)
            def _():
                state_out[turn] = dot_rows_wide(state_in[turn], joined_map) + joined_add[rows, :]

        @pl.when(place < places - 1)
        def _():
            relay(turn).start()

    start = state_in[...].reshape(width, width)
    states[head] = jnp.where(
        side == 0, start, dot_rows_wide(start, first[:, :width]) + first[:, width:].T
    )
    for step in range(1, chips):
        copy = state_copy(head, state_send.at[step], chip_at(step) * 2 + core)
        copy.start()
        sent.append(copy)
    copy = state_copy(head, state_send.at[0], twin)
    copy.start()
    sent.append(copy)

    def pass_on(chunk):
        for step in range(1, chips):
            slot = chip_at(step) * 2 + core
            copy = part_copy(slot, chunk, part_pass.at[chunk, step], twin)
            copy.wait_recv()
            copy.start()
            sent.append(copy)

    for chunk in range(chunks - 1):
        pass_on(chunk)

    loads[4].wait()
    loads[5].wait()
    gain = gain_out[...]
    share = jnp.full((2 * width, width), 1.0 / width, BF16)
    own_start = beside(*halves(states[head]))
    for chunk in range(chunks):
        mine[core, chunk] = settled(parts, head, chunk, own_start, gain, share)
    state_copy(twin, state_send.at[0], twin).wait_recv()
    twin_start = beside(*halves(states[twin]))
    for chunk in range(chunks):
        part_copy(twin, chunk, part_send.at[chunk, 0], twin).wait_recv()
        mine[1 - core, chunk] = settled(parts, twin, chunk, twin_start, gain, share)
    pass_on(chunks - 1)
    own_weights = w_out[pl.ds(pl.multiple_of(chip * 2 * width, 2 * width), 2 * width), :]
    for chunk in range(chunks):
        done[chunk] = dot(beside(mine[0, chunk], mine[1, chunk]), own_weights)

    for step in range(1, chips):
        slot = chip_at(step) * 2 + core
        copy = state_copy(slot, state_pass.at[step], twin)
        copy.wait_recv()
        copy.start()
        sent.append(copy)

    for chunk in range(chunks):
        for step in range(1, chips):
            slot = chip_at(step) * 2 + 1 - core
            part_copy(slot, chunk, part_pass.at[chunk, step], twin).wait_recv()
    for step in range(1, chips):
        slot = chip_at(step) * 2 + 1 - core
        state_copy(slot, state_pass.at[step], twin).wait_recv()

    for copy in sent:
        copy.wait_send()
    swap.wait_send()

    @pl.when(place < places - 1)
    def _():
        for turn in range(rounds):
            relay(turn).wait_send()


def finish(parts, states, gain_ref, w_ref, done, out_ref, staged, sems):
    heads, chunks = parts.shape[:2]
    size, width = parts.shape[3:]
    chip, chips = lax.axis_index("head") // 2, heads // 2
    gain = gain_ref[...]
    share = jnp.full((2 * width, width), 1.0 / width, BF16)
    slots = [lax.rem(chip + step, chips) * 2 + side for step in range(1, chips) for side in range(2)]
    starts = [beside(*halves(states[slot])) for slot in slots]
    weights = above(*[w_ref[pl.ds(pl.multiple_of(slot * width, width), width), :] for slot in slots])
    copies = []
    for chunk in range(chunks):
        rows = [
            settled(parts, slot, chunk, start, gain, share) for slot, start in zip(slots, starts)
        ]
        staged[chunk] = (done[chunk] + dot(beside(*rows), weights)).astype(BF16)
        copy = pltpu.make_async_copy(
            staged.at[chunk], out_ref.at[pl.ds(chunk * size, size), :], sems.at[chunk]
        )
        copy.start()
        copies.append(copy)
    for copy in copies:
        copy.wait()


def solution(mesh):
    count, heads = mesh.shape["ctx"], mesh.shape["head"]

    def shards(queries, keys, values, write_rates, norm_gain, w_out):
        length, width = queries.shape
        blocks = length // GROUP
        size = length // CHUNKS
        columns = w_out.shape[1]
        vmem = pl.BlockSpec(memory_space=pltpu.VMEM)
        hbm = pl.BlockSpec(memory_space=pltpu.MemorySpace.HBM)
        parts, states, gain, weights, done = pl.pallas_call(
            functools.partial(kernel, count, heads),
            out_shape=(
                jax.ShapeDtypeStruct((heads, CHUNKS, 2, size, width), BF16),
                jax.ShapeDtypeStruct((heads, width, width), F32),
                jax.ShapeDtypeStruct((1, width), F32),
                jax.ShapeDtypeStruct(w_out.shape, BF16),
                jax.ShapeDtypeStruct((CHUNKS, size, columns), F32),
            ),
            in_specs=[hbm] * 6,
            out_specs=(vmem,) * 5,
            scratch_shapes=[
                pltpu.VMEM((length, width), BF16),
                pltpu.VMEM((length, width), BF16),
                pltpu.VMEM((length, width), BF16),
                pltpu.VMEM((1, length), F32),
                pltpu.VMEM((blocks, GROUP, GROUP), BF16),
                pltpu.VMEM((blocks, GROUP, GROUP), BF16),
                pltpu.VMEM((blocks, GROUP, GROUP), F32),
                pltpu.VMEM((blocks, GROUP, 2 * width), F32),
                pltpu.VMEM((2, CHUNKS, size, width), BF16),
                pltpu.VMEM((2, GROUP, 2 * width), F32),
                pltpu.VMEM((ROUNDS, width // ROUNDS, width), F32),
                pltpu.VMEM((ROUNDS, width // ROUNDS, width), F32),
                pltpu.SemaphoreType.DMA((6,)),
                pltpu.SemaphoreType.DMA,
                pltpu.SemaphoreType.DMA,
                pltpu.SemaphoreType.DMA((ROUNDS,)),
                pltpu.SemaphoreType.DMA((ROUNDS,)),
                pltpu.SemaphoreType.DMA((CHUNKS, heads // 2)),
                pltpu.SemaphoreType.DMA((CHUNKS, heads // 2)),
                pltpu.SemaphoreType.DMA((CHUNKS, heads)),
                pltpu.SemaphoreType.DMA((heads // 2,)),
                pltpu.SemaphoreType.DMA((heads // 2,)),
                pltpu.SemaphoreType.DMA((heads,)),
            ],
            compiler_params=pltpu.CompilerParams(
                collective_id=0, has_side_effects=True, vmem_limit_bytes=24 << 20
            ),
        )(*[
            pltpu.with_memory_space_constraint(given, pltpu.MemorySpace.HBM)
            for given in (queries, keys, values, write_rates, norm_gain.reshape(1, width), w_out)
        ])
        return pl.pallas_call(
            finish,
            out_shape=jax.ShapeDtypeStruct((length, columns), BF16),
            in_specs=[vmem] * 5,
            out_specs=pl.BlockSpec(memory_space=pltpu.MemorySpace.HBM),
            scratch_shapes=[
                pltpu.VMEM((CHUNKS, size, columns), BF16),
                pltpu.SemaphoreType.DMA((CHUNKS,)),
            ],
            compiler_params=pltpu.CompilerParams(vmem_limit_bytes=24 << 20),
        )(parts, states, gain, weights, done)

    return jax.shard_map(
        shards,
        mesh=mesh,
        in_specs=(
            P("ctx", "head"),
            P("ctx", "head"),
            P("ctx", "head"),
            P("head", "ctx"),
            P(),
            P(None, "head"),
        ),
        out_specs=P("ctx", "head"),
        check_vma=False,
    )
```

```python
import functools

import jax
import jax.numpy as jnp
from jax import lax
from jax.experimental import pallas as pl
from jax.experimental.pallas import tpu as pltpu
from jax.sharding import PartitionSpec as P

F32 = jnp.float32
BF16 = jnp.bfloat16
MESH = pl.DeviceIdType.MESH
GROUP = 128
CHUNKS = 4
ROUNDS = 4


def halves(wide):
    high = wide.astype(BF16)
    return high, (wide - high.astype(F32)).astype(BF16)


def dot(left, right):
    return jnp.dot(left, right, preferred_element_type=F32)


def dot_rows(left, right):
    return lax.dot_general(left, right, (((1,), (1,)), ((), ())), preferred_element_type=F32)


def beside(*parts):
    return jnp.concatenate(parts, axis=1)


def above(*parts):
    return jnp.concatenate(parts, axis=0)


def dot_wide(left, right):
    left_high, left_low = halves(left)
    right_high, right_low = halves(right)
    return dot(beside(left_high, left_low, left_high), above(right_high, right_high, right_low))


def dot_rows_wide(left, right):
    left_high, left_low = halves(left)
    right_high, right_low = halves(right)
    return dot_rows(beside(left_high, left_low, left_high), beside(right_high, right_high, right_low))


def settled(parts, slot, chunk, start, gain, share):
    asked = parts[slot, chunk, 0]
    result = dot_rows(beside(asked, asked), start) + parts[slot, chunk, 1].astype(F32)
    power = dot(beside(*halves(result * result)), share)
    return (result * lax.rsqrt(power + 1e-06) * gain).astype(BF16)


def kernel(
    count,
    heads,
    q_hbm,
    k_hbm,
    v_hbm,
    rate_hbm,
    gain_hbm,
    w_hbm,
    parts,
    states,
    gain_out,
    w_out,
    done,
    q_ref,
    k_ref,
    v_ref,
    rate_ref,
    inverse,
    coarse,
    lower,
    writes,
    mine,
    pair,
    state_in,
    state_out,
    load_sem,
    pair_send,
    pair_recv,
    relay_send,
    relay_recv,
    part_send,
    part_pass,
    part_recv,
    state_send,
    state_pass,
    state_recv,
):
    ctx = lax.axis_index("ctx")
    head = lax.axis_index("head")
    side = lax.rem(ctx, 2)
    place = ctx // 2
    places = count // 2
    mate = ctx + 1 - 2 * side
    core = lax.rem(head, 2)
    chip = head // 2
    chips = heads // 2
    twin = head + 1 - 2 * core
    length, width = q_ref.shape
    blocks = length // GROUP
    chunks = parts.shape[1]
    size = length // chunks

    loads = [
        pltpu.make_async_copy(source, target, load_sem.at[at])
        for at, (source, target) in enumerate(
            (
                (k_hbm, k_ref),
                (rate_hbm, rate_ref),
                (v_hbm, v_ref),
                (q_hbm, q_ref),
                (w_hbm, w_out),
                (gain_hbm, gain_out),
            )
        )
    ]
    for load in loads:
        load.start()
    barrier = pltpu.get_barrier_semaphore()

    def greet(to_ctx, to_head):
        pl.semaphore_signal(barrier, inc=1, device_id=(to_ctx, to_head), device_id_type=MESH)

    def chip_at(step):
        return lax.rem(chip + step, chips)

    greet(mate, head)
    greet(ctx, twin)
    for step in range(1, chips):
        greet(ctx, chip_at(step) * 2 + core)

    @pl.when(place > 0)
    def _():
        greet(ctx - 2, head)

    @pl.when(place < places - 1)
    def _():
        greet(ctx + 2, head)

    row = lax.broadcasted_iota(jnp.int32, (GROUP, GROUP), 0)
    col = lax.broadcasted_iota(jnp.int32, (GROUP, GROUP), 1)
    eye = (row == col).astype(F32)

    loads[0].wait()
    loads[1].wait()
    rates = above(*[rate_ref[0:1, b * GROUP : (b + 1) * GROUP] for b in range(blocks)])
    rate_cols = rates.T
    key_rows = []
    moves = []

    def part(ref, b):
        return ref[b * GROUP : (b + 1) * GROUP, :]

    for b in range(blocks):
        key = part(k_ref, b)
        wide = key.astype(F32)
        gram = dot_rows(key, key)
        scale_col = lax.rsqrt(jnp.sum(wide * wide, axis=1, keepdims=True) + 1e-06)
        scale_row = lax.rsqrt(jnp.sum(gram * eye, axis=0, keepdims=True) + 1e-06)
        key_rows.append(scale_row)
        strict = jnp.where(
            row > col, gram * (rate_cols[:, b : b + 1] * scale_col) * scale_row, 0.0
        )
        lower[b] = strict
        coarse[b] = strict.astype(BF16)
        near = (row // 2 == col // 2) & (row != col)
        inverse[b] = (eye - jnp.where(near, strict, 0.0)).astype(BF16)

    span = 2
    while span < GROUP:
        corner = (
            ((row // (2 * span) == col // (2 * span)) & (row // span != col // span))
            .astype(F32)
            .astype(BF16)
        )
        spots = [slice(at, at + span) for at in range(span, GROUP, 2 * span)]
        if span < 16:
            spots = [slice(0, GROUP)]
        for b in range(blocks):
            held = inverse[b]
            rows = above(*[held[spot, :] for spot in spots])
            change = dot(dot(rows, coarse[b] * corner).astype(BF16), held).astype(BF16)
            rows = rows - change
            at = 0
            for spot in spots:
                tall = spot.stop - spot.start
                inverse[b, spot, :] = rows[at : at + tall, :]
                at += tall
        span *= 2

    loads[2].wait()
    for b in range(blocks):
        key = part(k_ref, b)
        value = part(v_ref, b)
        wide = key.astype(F32)
        scale_col = lax.rsqrt(jnp.sum(wide * wide, axis=1, keepdims=True) + 1e-06)
        held = inverse[b]
        high, low = halves(lower[b])
        miss = eye - held.astype(F32) - dot(beside(high, low), above(held, held))
        rough = miss.astype(BF16)
        miss = miss + dot(rough, rough)
        exact = held.astype(F32) + dot(held, miss.astype(BF16))
        spread = exact * rates[b : b + 1, :]
        key_high, key_low = halves(spread * key_rows[b])
        value_high, value_low = halves(spread)
        written = beside(
            dot(beside(key_high, key_low), above(key, key)),
            dot(beside(value_high, value_low), above(value, value)),
        )
        writes[b] = written
        high, low = halves(written * scale_col)
        turned = key.T
        moved = dot(beside(turned, turned), above(high, low))
        moves.append(beside(eye - moved[:, :width], moved[:, width:]))

    nothing = jnp.zeros((GROUP, width), F32)

    def after(later, earlier):
        return dot_wide(later[:, :width], earlier) + beside(nothing, later[:, width:])

    ranges = {(b, b + 1): moves[b] for b in range(blocks)}
    reach = 1
    while reach < blocks:
        for b in range(0, blocks, 2 * reach):
            middle, end = min(b + reach, blocks), min(b + 2 * reach, blocks)
            if middle < end:
                ranges[b, end] = after(ranges[middle, end], ranges[b, middle])
        reach *= 2
    pair[side] = ranges[0, blocks]

    pl.semaphore_wait(
        barrier,
        2
        + (chips - 1)
        + (place > 0).astype(jnp.int32)
        + (place < places - 1).astype(jnp.int32),
    )
    swap = pltpu.make_async_remote_copy(
        src_ref=pair.at[side],
        dst_ref=pair.at[side],
        send_sem=pair_send,
        recv_sem=pair_recv,
        device_id=(mate, head),
        device_id_type=MESH,
    )
    swap.start()

    loads[3].wait()
    for b in range(1, blocks):
        if (0, b) not in ranges:
            low = b & -b
            ranges[0, b] = after(ranges[b - low, b], ranges[0, b - low])

    def part_copy(slot, chunk, send_sem, to_head):
        return pltpu.make_async_remote_copy(
            src_ref=parts.at[slot, chunk],
            dst_ref=parts.at[slot, chunk],
            send_sem=send_sem,
            recv_sem=part_recv.at[chunk, slot],
            device_id=(ctx, to_head),
            device_id_type=MESH,
        )

    rounds = state_in.shape[0]
    tall = width // rounds

    def state_copy(slot, turn, send_sem, to_head):
        view = states.at[slot, pl.ds(turn * tall, tall), :]
        return pltpu.make_async_remote_copy(
            src_ref=view,
            dst_ref=view,
            send_sem=send_sem,
            recv_sem=state_recv.at[turn, slot],
            device_id=(ctx, to_head),
            device_id_type=MESH,
        )

    sent = []
    for b in range(blocks):
        query = part(q_ref, b)
        wide = query.astype(F32)
        scale_col = lax.rsqrt(jnp.sum(wide * wide, axis=1, keepdims=True) + 1e-06)
        scores = dot_rows(query, part(k_ref, b))
        scores = jnp.where(row >= col, scores * scale_col * key_rows[b], 0.0)
        seen = dot_wide(scores, writes[b])
        asked = wide * scale_col - seen[:, :width]
        if b == 0:
            both = beside(asked, nothing)
        else:
            both = dot_wide(asked, ranges[0, b])
        chunk, at = divmod(b * GROUP, size)
        parts[head, chunk, 0, at : at + GROUP, :] = both[:, :width].astype(BF16)
        parts[head, chunk, 1, at : at + GROUP, :] = (both[:, width:] + seen[:, width:]).astype(BF16)
        if at + GROUP == size:
            for step in range(1, chips):
                copy = part_copy(head, chunk, part_send.at[chunk, step], chip_at(step) * 2 + core)
                copy.start()
                sent.append(copy)
            copy = part_copy(head, chunk, part_send.at[chunk, 0], twin)
            copy.start()
            sent.append(copy)

    swap.wait_recv()
    first = pair[0]
    second = pair[1]
    joined = after(second, first)
    joined_map = joined[:, :width]
    joined_add = joined[:, width:].T
    first_map = first[:, :width]
    first_add = first[:, width:].T

    def relay(turn):
        return pltpu.make_async_remote_copy(
            src_ref=state_out.at[turn],
            dst_ref=state_in.at[turn],
            send_sem=relay_send.at[turn],
            recv_sem=relay_recv.at[turn],
            device_id=(lax.rem(ctx + 2, count), head),
            device_id_type=MESH,
        )

    for turn in range(rounds):
        rows = slice(turn * tall, (turn + 1) * tall)

        @pl.when(place == 0)
        def _():
            state_in[turn] = jnp.zeros((tall, width), F32)
            state_out[turn] = joined_add[rows, :]

        @pl.when(place > 0)
        def _():
            relay(turn).wait_recv()

            @pl.when(place < places - 1)
            def _():
                state_out[turn] = dot_rows_wide(state_in[turn], joined_map) + joined_add[rows, :]

        @pl.when(place < places - 1)
        def _():
            relay(turn).start()

        start = state_in[turn]
        states[head, rows, :] = jnp.where(
            side == 0, start, dot_rows_wide(start, first_map) + first_add[rows, :]
        )
        for step in range(1, chips):
            copy = state_copy(head, turn, state_send.at[turn, step], chip_at(step) * 2 + core)
            copy.start()
            sent.append(copy)
        copy = state_copy(head, turn, state_send.at[turn, 0], twin)
        copy.start()
        sent.append(copy)

    def pass_on(chunk):
        for step in range(1, chips):
            slot = chip_at(step) * 2 + core
            copy = part_copy(slot, chunk, part_pass.at[chunk, step], twin)
            copy.wait_recv()
            copy.start()
            sent.append(copy)

    for chunk in range(chunks - 1):
        pass_on(chunk)

    loads[4].wait()
    loads[5].wait()
    gain = gain_out[...]
    share = jnp.full((2 * width, width), 1.0 / width, BF16)
    own_start = beside(*halves(states[head]))
    for chunk in range(chunks):
        mine[core, chunk] = settled(parts, head, chunk, own_start, gain, share)
    for turn in range(rounds):
        state_copy(twin, turn, state_send.at[turn, 0], twin).wait_recv()
    twin_start = beside(*halves(states[twin]))
    for chunk in range(chunks):
        part_copy(twin, chunk, part_send.at[chunk, 0], twin).wait_recv()
        mine[1 - core, chunk] = settled(parts, twin, chunk, twin_start, gain, share)
    pass_on(chunks - 1)
    own_weights = w_out[pl.ds(pl.multiple_of(chip * 2 * width, 2 * width), 2 * width), :]
    for chunk in range(chunks):
        done[chunk] = dot(beside(mine[0, chunk], mine[1, chunk]), own_weights)

    for turn in range(rounds):
        for step in range(1, chips):
            slot = chip_at(step) * 2 + core
            copy = state_copy(slot, turn, state_pass.at[turn, step], twin)
            copy.wait_recv()
            copy.start()
            sent.append(copy)

    for chunk in range(chunks):
        for step in range(1, chips):
            slot = chip_at(step) * 2 + 1 - core
            part_copy(slot, chunk, part_pass.at[chunk, step], twin).wait_recv()
    for turn in range(rounds):
        for step in range(1, chips):
            slot = chip_at(step) * 2 + 1 - core
            state_copy(slot, turn, state_pass.at[turn, step], twin).wait_recv()

    for copy in sent:
        copy.wait_send()
    swap.wait_send()

    @pl.when(place < places - 1)
    def _():
        for turn in range(rounds):
            relay(turn).wait_send()


def finish(parts, states, gain_ref, w_ref, done, out_ref, staged, sems):
    heads, chunks = parts.shape[:2]
    size, width = parts.shape[3:]
    chip, chips = lax.axis_index("head") // 2, heads // 2
    gain = gain_ref[...]
    share = jnp.full((2 * width, width), 1.0 / width, BF16)
    slots = [lax.rem(chip + step, chips) * 2 + side for step in range(1, chips) for side in range(2)]
    starts = [beside(*halves(states[slot])) for slot in slots]
    weights = above(*[w_ref[pl.ds(pl.multiple_of(slot * width, width), width), :] for slot in slots])
    copies = []
    for chunk in range(chunks):
        rows = [
            settled(parts, slot, chunk, start, gain, share) for slot, start in zip(slots, starts)
        ]
        staged[chunk] = (done[chunk] + dot(beside(*rows), weights)).astype(BF16)
        copy = pltpu.make_async_copy(
            staged.at[chunk], out_ref.at[pl.ds(chunk * size, size), :], sems.at[chunk]
        )
        copy.start()
        copies.append(copy)
    for copy in copies:
        copy.wait()


def solution(mesh):
    count, heads = mesh.shape["ctx"], mesh.shape["head"]

    def shards(queries, keys, values, write_rates, norm_gain, w_out):
        length, width = queries.shape
        blocks = length // GROUP
        size = length // CHUNKS
        columns = w_out.shape[1]
        vmem = pl.BlockSpec(memory_space=pltpu.VMEM)
        hbm = pl.BlockSpec(memory_space=pltpu.MemorySpace.HBM)
        parts, states, gain, weights, done = pl.pallas_call(
            functools.partial(kernel, count, heads),
            out_shape=(
                jax.ShapeDtypeStruct((heads, CHUNKS, 2, size, width), BF16),
                jax.ShapeDtypeStruct((heads, width, width), F32),
                jax.ShapeDtypeStruct((1, width), F32),
                jax.ShapeDtypeStruct(w_out.shape, BF16),
                jax.ShapeDtypeStruct((CHUNKS, size, columns), F32),
            ),
            in_specs=[hbm] * 6,
            out_specs=(vmem,) * 5,
            scratch_shapes=[
                pltpu.VMEM((length, width), BF16),
                pltpu.VMEM((length, width), BF16),
                pltpu.VMEM((length, width), BF16),
                pltpu.VMEM((1, length), F32),
                pltpu.VMEM((blocks, GROUP, GROUP), BF16),
                pltpu.VMEM((blocks, GROUP, GROUP), BF16),
                pltpu.VMEM((blocks, GROUP, GROUP), F32),
                pltpu.VMEM((blocks, GROUP, 2 * width), F32),
                pltpu.VMEM((2, CHUNKS, size, width), BF16),
                pltpu.VMEM((2, GROUP, 2 * width), F32),
                pltpu.VMEM((ROUNDS, width // ROUNDS, width), F32),
                pltpu.VMEM((ROUNDS, width // ROUNDS, width), F32),
                pltpu.SemaphoreType.DMA((6,)),
                pltpu.SemaphoreType.DMA,
                pltpu.SemaphoreType.DMA,
                pltpu.SemaphoreType.DMA((ROUNDS,)),
                pltpu.SemaphoreType.DMA((ROUNDS,)),
                pltpu.SemaphoreType.DMA((CHUNKS, heads // 2)),
                pltpu.SemaphoreType.DMA((CHUNKS, heads // 2)),
                pltpu.SemaphoreType.DMA((CHUNKS, heads)),
                pltpu.SemaphoreType.DMA((ROUNDS, heads // 2)),
                pltpu.SemaphoreType.DMA((ROUNDS, heads // 2)),
                pltpu.SemaphoreType.DMA((ROUNDS, heads)),
            ],
            compiler_params=pltpu.CompilerParams(
                collective_id=0, has_side_effects=True, vmem_limit_bytes=24 << 20
            ),
        )(*[
            pltpu.with_memory_space_constraint(given, pltpu.MemorySpace.HBM)
            for given in (queries, keys, values, write_rates, norm_gain.reshape(1, width), w_out)
        ])
        return pl.pallas_call(
            finish,
            out_shape=jax.ShapeDtypeStruct((length, columns), BF16),
            in_specs=[vmem] * 5,
            out_specs=pl.BlockSpec(memory_space=pltpu.MemorySpace.HBM),
            scratch_shapes=[
                pltpu.VMEM((CHUNKS, size, columns), BF16),
                pltpu.SemaphoreType.DMA((CHUNKS,)),
            ],
            compiler_params=pltpu.CompilerParams(vmem_limit_bytes=24 << 20),
        )(parts, states, gain, weights, done)

    return jax.shard_map(
        shards,
        mesh=mesh,
        in_specs=(
            P("ctx", "head"),
            P("ctx", "head"),
            P("ctx", "head"),
            P("head", "ctx"),
            P(),
            P(None, "head"),
        ),
        out_specs=P("ctx", "head"),
        check_vma=False,
    )
```
